128 devices in a mesh: sx: 8 (over y, core), sy: 16 (over x, z).
Axes of the slice: x: 4, y: 4, z: 4, core: 2. Of those that a mesh axis runs over, the one named last changes fastest.
Arguments:
- loads: float32 [8, 16, 1536, 256], P('sx', 'sy')
- schur_flex: float32 [8, 16, 1536, 1536], P('sx', 'sy'), as said below
- dirichlet: float32 [8, 16, 1536, 1536], P('sx', 'sy'), as said below
- coupling: float32 [8, 16, 16, 1536], P('sx', 'sy'), may hold values from -0.3125 to 0.3125
- corner_index: int32 [8, 16, 16], P('sx', 'sy'), may hold values from 0 to 512, as said below
- face_lists: int32 [8, 16, 4, 384], P('sx', 'sy'), may hold values from 0 to 383, as said below
- coarse_inverse: float32 [512, 512], P(('sx', 'sy')), as said below
Outputs:
- multipliers: float32 [8, 16, 1536, 256], P('sx', 'sy')
- residual: float32 [8, 16, 1536, 256], P('sx', 'sy')
The draws below stay inside these ranges and needn't reach their ends.
Inputs may be any that keep to these rules, and one draw needn't show every extreme that they name: `corner_index`: each subdomain lists 4 coarse dofs for each of its four corners; 512 marks a corner on the clamped edges of the panel, which has no coarse dof; every coarse dof below 512 is named by some subdomain. `face_lists`: each face's list is a permutation of the 384 dofs of the facing face; the facing lists of two neighbouring subdomains are inverse permutations. `schur_flex`: symmetric positive definite for every subdomain. `dirichlet`: symmetric positive definite for every subdomain. `coarse_inverse`: symmetric positive definite.
All inputs are finite; a program needn't handle non-finite values.
Results may differ from the reference program's by a relative error of at most 0.00017.
Values sent between devices are 32-bit elements; how exact they have to be, the bound alone decides.
A program may use at most 128 MiB of HBM per device.

```python
import math
import jax
import jax.numpy as jnp
from jax import lax

NI = 1536
LOADS = 256
CDOF = 4
ITERS = 2
FACE = 384
NCL = 16
GLOBAL_SYS_SIZE = 512
N_SX = 8
N_SY = 16


def spd_block(key, order):
    first, second = jax.random.split(key, 2)
    offdiag = jax.random.uniform(first, (order, order), jnp.float32, -1.0, 1.0) / math.sqrt(order)
    symmetric = 0.5 * (offdiag + offdiag.T)
    identity = jnp.eye(order, dtype=jnp.float32)
    diagonal = jax.random.uniform(second, (order,), jnp.float32, 1.05, 2.0)
    matrix = symmetric * (1.0 - identity) + identity * diagonal[:, None]
    return matrix


def interface_block(key):
    return spd_block(key, NI)


def spd_stack(key, salt):
    keys = jax.random.split(jax.random.fold_in(key, salt), N_SX * N_SY)
    return lax.map(interface_block, keys).reshape(N_SX, N_SY, NI, NI)


def draw_schur_flex(key, part):
    return spd_stack(key, 101)


def draw_dirichlet(key, part):
    return spd_stack(key, 202)


def draw_coarse_inverse(key, part):
    return spd_block(jax.random.fold_in(key, 303), GLOBAL_SYS_SIZE)


def draw_loads(key, part):
    first = jax.random.fold_in(jax.random.fold_in(key, 404), 0)
    devices = N_SX * N_SY
    position = jnp.arange(devices, dtype=jnp.float32).reshape(N_SX, N_SY, 1, 1) / (devices - 1)
    values = jax.random.normal(first, (N_SX, N_SY, NI, LOADS), jnp.float32)
    return values * (1.0 + 2.0 * position)


def inverse_perm(perm):
    return jnp.zeros(perm.shape, jnp.int32).at[perm].set(jnp.arange(perm.shape[0], dtype=jnp.int32))


def face_perm(key):
    return jax.random.permutation(key, FACE).astype(jnp.int32)


def draw_face_lists(key, part):
    keys = jax.random.split(jax.random.fold_in(key, 505), 2 * N_SX * N_SY)
    along_x = jax.vmap(face_perm)(keys[:N_SX * N_SY]).reshape(N_SX, N_SY, FACE)
    along_y = jax.vmap(face_perm)(keys[N_SX * N_SY:]).reshape(N_SX, N_SY, FACE)
    invert = jax.vmap(jax.vmap(inverse_perm))
    face_zero = invert(jnp.roll(along_x, 1, axis=0))
    face_two = invert(jnp.roll(along_y, 1, axis=1))
    return jnp.stack([face_zero, along_x, face_two, along_y], axis=2).astype(jnp.int32)


def draw_corner_index(key, part):
    relabel_unknowns = jax.random.permutation(jax.random.fold_in(key, 606), GLOBAL_SYS_SIZE).astype(jnp.int32)
    index_a = jnp.arange(N_SX, dtype=jnp.int32)[:, None, None]
    index_b = jnp.arange(N_SY, dtype=jnp.int32)[None, :, None]
    local = jnp.arange(NCL, dtype=jnp.int32)[None, None, :]
    junction_point = local // CDOF
    component = local % CDOF
    vertex_a = index_a + junction_point // 2
    vertex_b = index_b + junction_point % 2
    genuine_elements = (vertex_a < N_SX) & (vertex_b < N_SY)
    grid_node = (vertex_a * N_SY + vertex_b) * CDOF + component
    grid_node = jnp.minimum(grid_node, GLOBAL_SYS_SIZE - 1)
    return jnp.where(genuine_elements, relabel_unknowns[grid_node], GLOBAL_SYS_SIZE).astype(jnp.int32)


def steps_of(own_key, shape, pieces, low, top_value):
    gain = 1.0
    for axis_at, shards_of in pieces:
        heights = jax.random.uniform(jax.random.fold_in(jax.random.fold_in(own_key, 6), axis_at), (shards_of,), jnp.float32, low / len(pieces), top_value / len(pieces))
        gain = gain * jnp.repeat(jnp.exp(heights), shape[axis_at] // shards_of).reshape((-1,) + (1,) * (len(shape) - 1 - axis_at))
    return gain


def centred(stream_key, extent, scale, bound, pieces=(), kind=jnp.bfloat16):
    gain = steps_of(stream_key, extent, pieces, -0.22, 0.18) if pieces else 1.0
    drawn = jax.random.normal(stream_key, extent, jnp.float32) * scale * gain
    return jnp.minimum(jnp.maximum(drawn, -bound), bound).astype(kind)


def setup_inputs(seed: int = 0) -> dict:
    seeds = jax.random.split(jax.random.key(seed), 8)
    loads = draw_loads(jax.random.fold_in(seeds[7], 71), 0)
    schur_flex = draw_schur_flex(jax.random.fold_in(seeds[7], 71), 0)
    dirichlet = draw_dirichlet(jax.random.fold_in(seeds[7], 71), 0)
    coupling = centred(seeds[3], (N_SX, N_SY, NCL, NI), (NI // 4) ** -0.5, 0.3125, ((0, 8), (1, 16)), jnp.float32)
    corner_index = draw_corner_index(jax.random.fold_in(seeds[7], 71), 0)
    face_lists = draw_face_lists(jax.random.fold_in(seeds[7], 71), 0)
    coarse_inverse = draw_coarse_inverse(jax.random.fold_in(seeds[7], 71), 0)
    return dict(loads=loads, schur_flex=schur_flex, dirichlet=dirichlet, coupling=coupling, corner_index=corner_index, face_lists=face_lists, coarse_inverse=coarse_inverse)


def subdomain_product(pair):
    return jnp.dot(pair[0], pair[1], precision=lax.Precision.HIGHEST)


def batched_product(matrices, vectors):
    size = matrices.shape[2]
    final_result = lax.map(subdomain_product, (matrices.reshape(-1, size, size), vectors.reshape(-1, size, LOADS)))
    return final_result.reshape(N_SX, N_SY, size, LOADS)


def jump(field, face_lists):
    face_rows = field.reshape(N_SX, N_SY, 4, FACE, LOADS)
    zero_x = jnp.zeros((1, N_SY, FACE, LOADS), field.dtype)
    zero_y = jnp.zeros((N_SX, 1, FACE, LOADS), field.dtype)
    from_low_x = jnp.concatenate([zero_x, face_rows[:-1, :, 1]], axis=0)
    from_high_x = jnp.concatenate([face_rows[1:, :, 0], zero_x], axis=0)
    from_low_y = jnp.concatenate([zero_y, face_rows[:, :-1, 3]], axis=1)
    from_high_y = jnp.concatenate([face_rows[:, 1:, 2], zero_y], axis=1)
    received = jnp.stack([from_low_x, from_high_x, from_low_y, from_high_y], axis=2)
    index_a = jnp.arange(N_SX, dtype=jnp.int32)[:, None, None, None]
    index_b = jnp.arange(N_SY, dtype=jnp.int32)[None, :, None, None]
    index_f = jnp.arange(4, dtype=jnp.int32)[None, None, :, None]
    matched = received[index_a, index_b, index_f, face_lists]
    return (face_rows - matched).reshape(N_SX, N_SY, NI, LOADS)


def apply_dual(dual_vector, schur_flex, coupling, corner_index, face_lists, coarse_inverse):
    highest = lax.Precision.HIGHEST
    spread = jump(dual_vector, face_lists)
    fine_part = batched_product(schur_flex, spread)
    local_load = jnp.einsum("abki,abir->abkr", coupling, spread, precision=highest)
    coarse_rhs = jnp.zeros((GLOBAL_SYS_SIZE, LOADS), jnp.float32).at[corner_index.reshape(-1)].add(local_load.reshape(-1, LOADS), mode="drop")
    coarse_sol = jnp.dot(coarse_inverse, coarse_rhs, precision=highest)
    filled_out = jnp.concatenate([coarse_sol, jnp.zeros((1, LOADS), jnp.float32)], axis=0)
    picked = filled_out[corner_index]
    correction = jnp.einsum("abki,abkr->abir", coupling, picked, precision=highest)
    return jump(fine_part + correction, face_lists)


def precondition(dual_vector, dirichlet, face_lists):
    spread = jump(dual_vector, face_lists)
    operator_applied = batched_product(dirichlet, spread)
    return 0.5 * jump(operator_applied, face_lists)


def inner(first, second):
    return jnp.sum(first * second, axis=(0, 1, 2))


def reference(loads, schur_flex, dirichlet, coupling, corner_index, face_lists, coarse_inverse):
    force_discontinuity = jump(loads, face_lists)
    multipliers = jnp.zeros_like(force_discontinuity)
    residual = force_discontinuity
    precond = precondition(residual, dirichlet, face_lists)
    direction = precond
    residual_inner = inner(residual, precond)
    for iteration in range(ITERS):
        image = apply_dual(direction, schur_flex, coupling, corner_index, face_lists, coarse_inverse)
        step_size = residual_inner / inner(direction, image)
        multipliers = multipliers + step_size * direction
        residual = residual - step_size * image
        if iteration + 1 < ITERS:
            precond = precondition(residual, dirichlet, face_lists)
            new_dot = inner(residual, precond)
            direction = precond + (new_dot / residual_inner) * direction
            residual_inner = new_dot
    return multipliers, residual
```

```python
import jax
import jax.numpy as jnp
from jax import lax
from jax.sharding import PartitionSpec as P

ITERS = 2


def shifted(block, axis, distance):
    devices = range(lax.axis_size(axis))
    route = [(i - distance, i) for i in devices if i - distance in devices]
    return lax.ppermute(block, axis, route)


def jump(field, face_index):
    size = field.shape[0] // 4
    width = field.shape[1]
    face_rows = field.reshape(4, size, width)
    from_low_x = shifted(face_rows[1], "sx", 1)
    from_high_x = shifted(face_rows[0], "sx", -1)
    from_low_y = shifted(face_rows[3], "sy", 1)
    from_high_y = shifted(face_rows[2], "sy", -1)
    received = jnp.stack([from_low_x, from_high_x, from_low_y, from_high_y], axis=0)
    matched = received[jnp.arange(4, dtype=jnp.int32)[:, None], face_index]
    return (face_rows - matched).reshape(4 * size, width)


def coarse_solve(coarse_rhs, stiffness_inverse_lines):
    highest = lax.Precision.HIGHEST
    total = lax.psum(coarse_rhs, ("sx", "sy"))
    mine = jnp.dot(stiffness_inverse_lines, total, precision=highest)
    return lax.all_gather(mine, ("sx", "sy"), axis=0, tiled=True)


def inner(first, second):
    return jnp.sum(first * second, axis=0)


def shards(loads, schur_flex, dirichlet, coupling, corner_index, face_lists, coarse_inverse):
    high = lax.Precision.HIGH
    highest = lax.Precision.HIGHEST
    flex_mat = schur_flex[0, 0]
    prec_mat = dirichlet[0, 0]
    coupling_mat = coupling[0, 0]
    corners = corner_index[0, 0]
    face_index = face_lists[0, 0]
    ncoarse = coarse_inverse.shape[1]
    onehot = (corners[None, :] == jnp.arange(ncoarse, dtype=jnp.int32)[:, None]).astype(jnp.float32)
    size = face_index.shape[1]
    sx = lax.axis_index("sx")
    sy = lax.axis_index("sy")
    inside = jnp.stack([sx > 0, sx < lax.axis_size("sx") - 1, sy > 0, sy < lax.axis_size("sy") - 1])
    scale = jnp.repeat(1.0 + inside.astype(jnp.float32), size)[:, None]

    def total(values):
        return lax.psum(values, ("sx", "sy"))

    residual = jump(loads[0, 0], face_index)
    multipliers = jnp.zeros_like(residual)
    direction = None
    residual_inner = None
    for iteration in range(ITERS):
        spread = scale * residual
        operator_applied = jnp.dot(prec_mat, spread, precision=high)
        new_dot = total(0.5 * inner(spread, operator_applied))
        precond = 0.5 * jump(operator_applied, face_index)
        direction = precond if iteration == 0 else precond + new_dot / residual_inner * direction
        residual_inner = new_dot
        apply_spread = scale * direction
        fine_part = jnp.dot(flex_mat, apply_spread, precision=high)
        local_load = jnp.dot(coupling_mat, apply_spread, precision=high)
        coarse_rhs = jnp.dot(onehot, local_load, precision=highest)
        coarse_sol = coarse_solve(coarse_rhs, coarse_inverse)
        filled_out = jnp.concatenate([coarse_sol, jnp.zeros((1, direction.shape[1]), jnp.float32)], axis=0)
        picked = filled_out[corners]
        correction = lax.dot_general(
            coupling_mat, picked, (((0,), (0,)), ((), ())), precision=high
        )
        applied = fine_part + correction
        step_size = residual_inner / total(inner(apply_spread, applied))
        image_dir = jump(applied, face_index)
        multipliers = multipliers + step_size * direction
        residual = residual - step_size * image_dir
    return (multipliers[None, None], residual[None, None])


def solution(mesh):
    return jax.shard_map(
        shards,
        mesh=mesh,
        in_specs=(
            P("sx", "sy", None, None),
            P("sx", "sy", None, None),
            P("sx", "sy", None, None),
            P("sx", "sy", None, None),
            P("sx", "sy", None),
            P("sx", "sy", None, None),
            P(("sx", "sy"), None),
        ),
        out_specs=(P("sx", "sy", None, None), P("sx", "sy", None, None)),
        check_vma=False,
    )
```

```python
import jax
import jax.numpy as jnp
from jax import lax
from jax.sharding import PartitionSpec as P

HIGH = lax.Precision.HIGH
HIGHEST = lax.Precision.HIGHEST


def shifted(block, axis, distance):
    devices = range(lax.axis_size(axis))
    route = [(i - distance, i) for i in devices if i - distance in devices]
    return lax.ppermute(block, axis, route)


def facing(faces):
    return (
        shifted(faces[1], "sx", 1),
        shifted(faces[0], "sx", -1),
        shifted(faces[3], "sy", 1),
        shifted(faces[2], "sy", -1),
    )


def jump(field, match):
    size = field.shape[0] // 4
    faces = [field[f * size : (f + 1) * size] for f in range(4)]
    received = facing(faces)
    return jnp.concatenate(
        [faces[f] - jnp.dot(match[f], received[f], precision=HIGHEST) for f in range(4)], axis=0
    )


def inner(first, second):
    return jnp.sum(first * second, axis=0)


def shards(loads, schur_flex, dirichlet, coupling, corner_index, face_lists, coarse_inverse):
    flex_mat = schur_flex[0, 0]
    prec_mat = dirichlet[0, 0]
    coupling_mat = coupling[0, 0]
    corners = corner_index[0, 0]
    face_index = face_lists[0, 0]
    ncoarse = coarse_inverse.shape[1]
    ncl = corners.shape[0]
    size = face_index.shape[1]
    sx = lax.axis_index("sx")
    sy = lax.axis_index("sy")
    inside = jnp.stack([sx > 0, sx < lax.axis_size("sx") - 1, sy > 0, sy < lax.axis_size("sy") - 1])
    scale = jnp.repeat(1.0 + inside.astype(jnp.float32), size)[:, None]
    match = (face_index[:, :, None] == jnp.arange(size, dtype=jnp.int32)[None, None, :]).astype(jnp.float32)
    inverse = lax.all_gather(coarse_inverse, ("sx", "sy"), axis=0, tiled=True)

    slots = jnp.concatenate([corners, jnp.arange(ncoarse + 1, ncoarse + 4, dtype=jnp.int32)])
    place = (slots[None, :] == jnp.arange(ncoarse + 8, dtype=jnp.int32)[:, None]).astype(jnp.float32)

    coarse_ids = jnp.arange(ncoarse, dtype=jnp.float32)[None, :]
    own = corners.astype(jnp.float32)
    parts = [coupling_mat[:, f * size : (f + 1) * size].T for f in range(4)]
    tagged = [jnp.concatenate([part, jnp.broadcast_to(own, (8, ncl))], axis=0) for part in parts]
    pick = (own[:, None] == coarse_ids).astype(jnp.float32)
    columns = []
    for f, got in enumerate(facing(tagged)):
        their_pick = (got[size][:, None] == coarse_ids).astype(jnp.float32)
        theirs = jnp.dot(match[f], got[:size], precision=HIGHEST)
        columns.append(
            jnp.dot(parts[f], pick, precision=HIGHEST) - jnp.dot(theirs, their_pick, precision=HIGHEST)
        )
    coupling_jump = jnp.concatenate(columns, axis=0)

    def reduced(local_load, *rows):
        rows = list(rows) + [jnp.zeros_like(rows[0])] * (3 - len(rows))
        block = jnp.concatenate([local_load] + [row[None] for row in rows], axis=0)
        total = lax.psum(jnp.dot(place, block, precision=HIGHEST), ("sx", "sy"))
        return total[:ncoarse], total[ncoarse + 1], total[ncoarse + 2], total[ncoarse + 3]

    def coarse(rhs):
        sol = jnp.dot(inverse, rhs, precision=HIGHEST)
        return jnp.dot(coupling_jump, sol, precision=HIGHEST), inner(rhs, sol)

    def precondition(residual):
        spread = scale * residual
        applied = jnp.dot(prec_mat, spread, precision=HIGH)
        return 0.5 * jump(applied, match), 0.5 * inner(spread, applied)

    def flexible(direction):
        spread = scale * direction
        return spread, jnp.dot(flex_mat, spread, precision=HIGH), jnp.dot(coupling_mat, spread, precision=HIGH)

    residual = jump(loads[0, 0], match)
    direction, dot_part = precondition(residual)
    spread, flexed, load = flexible(direction)
    rhs, res_dot, energy, _ = reduced(load, dot_part, inner(spread, flexed))
    image = jump(flexed, match)
    correction, coarse_energy = coarse(rhs)
    step = res_dot / (energy + coarse_energy)
    residual = residual - step * (image + correction)
    multipliers = step * direction

    precond, dot_part = precondition(residual)
    spread, new_flexed, load = flexible(precond)
    new_rhs, new_dot, new_energy, cross = reduced(
        load, dot_part, inner(spread, new_flexed), inner(spread, flexed)
    )
    new_image = jump(new_flexed, match)
    beta = new_dot / res_dot
    rhs = new_rhs + beta * rhs
    energy = new_energy + beta * (2.0 * cross + beta * energy)
    correction, coarse_energy = coarse(rhs)
    step = new_dot / (energy + coarse_energy)
    multipliers = multipliers + step * (precond + beta * direction)
    residual = residual - step * (new_image + beta * image + correction)
    return (multipliers[None, None], residual[None, None])


def solution(mesh):
    return jax.shard_map(
        shards,
        mesh=mesh,
        in_specs=(
            P("sx", "sy", None, None),
            P("sx", "sy", None, None),
            P("sx", "sy", None, None),
            P("sx", "sy", None, None),
            P("sx", "sy", None),
            P("sx", "sy", None, None),
            P(("sx", "sy"), None),
        ),
        out_specs=(P("sx", "sy", None, None), P("sx", "sy", None, None)),
        check_vma=False,
    )
```

```python
import jax
import jax.numpy as jnp
from jax import lax
from jax.experimental import pallas as pl
from jax.experimental.pallas import tpu as pltpu
from jax.sharding import PartitionSpec as P

HIGH = lax.Precision.HIGH
HIGHEST = lax.Precision.HIGHEST


def shifted(block, axis, distance):
    devices = range(lax.axis_size(axis))
    route = [(i - distance, i) for i in devices if i - distance in devices]
    return lax.ppermute(block, axis, route)


def facing(faces):
    return (
        shifted(faces[1], "sx", 1),
        shifted(faces[0], "sx", -1),
        shifted(faces[3], "sy", 1),
        shifted(faces[2], "sy", -1),
    )


def jump(field, match):
    size = field.shape[0] // 4
    faces = [field[f * size : (f + 1) * size] for f in range(4)]
    received = facing(faces)
    return jnp.concatenate(
        [faces[f] - jnp.dot(match[f], received[f], precision=HIGHEST) for f in range(4)], axis=0
    )


def inner(first, second):
    return jnp.sum(first * second, axis=0)


def gather_kernel(block_ref, out_ref, held, send, recv, local):
    sx = lax.axis_index("sx")
    sy = lax.axis_index("sy")
    y, core = sx // 2, sx % 2
    x, z = sy // 4, sy % 4
    above, below, across = (y + 1) % 4, (y + 3) % 4, (y + 2) % 4
    sibling = (y * 2 + 1 - core, sy)
    along_x = [(sx, ((x + k) % 4) * 4 + z) for k in (1, 2, 3)]
    along_z = [(sx, x * 4 + (z + k) % 4) for k in (1, 2, 3)]
    up, down = (above * 2 + core, sy), (below * 2 + core, sy)

    partners = along_x + along_z + [up, down, sibling]
    barrier = pltpu.get_barrier_semaphore()
    for device in partners:
        pl.semaphore_signal(barrier, inc=1, device_id=device, device_id_type=pl.DeviceIdType.MESH)
    pl.semaphore_wait(barrier, len(partners))

    started = []

    def push(source, target, device):
        slot = len(started)
        copy = pltpu.make_async_remote_copy(
            src_ref=source,
            dst_ref=target,
            send_sem=send.at[slot],
            recv_sem=recv.at[slot],
            device_id=device,
            device_id_type=pl.DeviceIdType.MESH,
        )
        copy.start()
        started.append(copy)
        return copy

    keep = pltpu.make_async_copy(block_ref, held.at[core, y, z, x], local.at[0])
    keep.start()
    for copy in [push(block_ref, held.at[core, y, z, x], device) for device in along_x]:
        copy.wait_recv()
    keep.wait()
    row = held.at[core, y, z]
    for copy in [push(row, row, device) for device in along_z]:
        copy.wait_recv()
    plane = held.at[core, y]
    from_below = push(plane, plane, up)
    from_above = push(plane, plane, down)
    others = [push(plane, plane, sibling)]
    from_below.wait_recv()
    half = held.at[core, below, pl.ds(0, 2)]
    first = push(half, half, up)
    plane = held.at[core, below]
    others.append(push(plane, plane, sibling))
    from_above.wait_recv()
    half = held.at[core, above, pl.ds(2, 2)]
    second = push(half, half, down)
    plane = held.at[core, above]
    others.append(push(plane, plane, sibling))
    first.wait_recv()
    second.wait_recv()
    plane = held.at[core, across]
    others.append(push(plane, plane, sibling))
    for copy in others:
        copy.wait_recv()
    out = pltpu.make_async_copy(held, out_ref, local.at[1])
    out.start()
    out.wait()
    for copy in started:
        copy.wait_send()


def gathered(block):
    shape = (2, 4, 4, 4) + block.shape
    copies = 14
    return pl.pallas_call(
        gather_kernel,
        out_shape=jax.ShapeDtypeStruct(shape, block.dtype),
        in_specs=[pl.BlockSpec(memory_space=pltpu.VMEM)],
        out_specs=pl.BlockSpec(memory_space=pl.ANY),
        scratch_shapes=[
            pltpu.VMEM(shape, block.dtype),
            pltpu.SemaphoreType.DMA((copies,)),
            pltpu.SemaphoreType.DMA((copies,)),
            pltpu.SemaphoreType.DMA((2,)),
        ],
        compiler_params=pltpu.CompilerParams(collective_id=0, has_side_effects=True),
        cost_estimate=pl.CostEstimate(flops=0, bytes_accessed=100_000_000, transcendentals=0),
    )(block)


def shards(loads, schur_flex, dirichlet, coupling, corner_index, face_lists, coarse_inverse):
    flex_mat = schur_flex[0, 0]
    prec_mat = dirichlet[0, 0]
    coupling_mat = coupling[0, 0]
    corners = corner_index[0, 0]
    face_index = face_lists[0, 0]
    ncoarse = coarse_inverse.shape[1]
    ncl = corners.shape[0]
    size = face_index.shape[1]
    sx = lax.axis_index("sx")
    sy = lax.axis_index("sy")
    inside = jnp.stack([sx > 0, sx < lax.axis_size("sx") - 1, sy > 0, sy < lax.axis_size("sy") - 1])
    scale = jnp.repeat(1.0 + inside.astype(jnp.float32), size)[:, None]
    match = (face_index[:, :, None] == jnp.arange(size, dtype=jnp.int32)[None, None, :]).astype(jnp.float32)
    mine = jnp.pad(corners.astype(jnp.float32), (0, ncoarse - ncl))[None]
    everyone = lax.all_gather(jnp.concatenate([coarse_inverse, mine], axis=0), ("sx", "sy"), axis=0)
    inverse = everyone[:, :-1].reshape(ncoarse, ncoarse)

    listed = everyone[:, -1, :ncl].reshape(4, 2, 4, 4, ncl).transpose(1, 0, 3, 2, 4).reshape(-1, ncl)
    extra = jnp.array([1, 2, 3, 0, 0, 0, 0, 0], jnp.float32) + ncoarse
    slots = jnp.concatenate([listed, jnp.broadcast_to(extra, (listed.shape[0], 8))], axis=1).reshape(-1)
    place = (slots[None, :] == jnp.arange(ncoarse + 8, dtype=jnp.float32)[:, None]).astype(jnp.float32)

    coarse_ids = jnp.arange(ncoarse, dtype=jnp.float32)[None, :]
    own = corners.astype(jnp.float32)
    parts = [coupling_mat[:, f * size : (f + 1) * size].T for f in range(4)]
    tagged = [jnp.concatenate([part, jnp.broadcast_to(own, (8, ncl))], axis=0) for part in parts]
    pick = (own[:, None] == coarse_ids).astype(jnp.float32)
    columns = []
    for f, got in enumerate(facing(tagged)):
        their_pick = (got[size][:, None] == coarse_ids).astype(jnp.float32)
        theirs = jnp.dot(match[f], got[:size], precision=HIGHEST)
        columns.append(
            jnp.dot(parts[f], pick, precision=HIGHEST) - jnp.dot(theirs, their_pick, precision=HIGHEST)
        )
    coupling_jump = jnp.concatenate(columns, axis=0)

    def reduced(local_load, *rows):
        rows = list(rows) + [jnp.zeros_like(rows[0])] * (8 - len(rows))
        block = jnp.concatenate([local_load] + [row[None] for row in rows], axis=0)
        blocks = gathered(block).reshape(-1, block.shape[1])
        total = jnp.dot(place, blocks, precision=HIGHEST)
        return total[:ncoarse], total[ncoarse + 1], total[ncoarse + 2], total[ncoarse + 3]

    def coarse(rhs):
        sol = jnp.dot(inverse, rhs, precision=HIGHEST)
        return jnp.dot(coupling_jump, sol, precision=HIGHEST), inner(rhs, sol)

    def precondition(residual):
        spread = scale * residual
        applied = jnp.dot(prec_mat, spread, precision=HIGH)
        return 0.5 * jump(applied, match), 0.5 * inner(spread, applied)

    def flexible(direction):
        spread = scale * direction
        return spread, jnp.dot(flex_mat, spread, precision=HIGH), jnp.dot(coupling_mat, spread, precision=HIGH)

    residual = jump(loads[0, 0], match)
    direction, dot_part = precondition(residual)
    spread, flexed, load = flexible(direction)
    rhs, res_dot, energy, _ = reduced(load, dot_part, inner(spread, flexed))
    image = jump(flexed, match)
    correction, coarse_energy = coarse(rhs)
    step = res_dot / (energy + coarse_energy)
    residual = residual - step * (image + correction)
    multipliers = step * direction

    precond, dot_part = precondition(residual)
    spread, new_flexed, load = flexible(precond)
    new_rhs, new_dot, new_energy, cross = reduced(
        load, dot_part, inner(spread, new_flexed), inner(spread, flexed)
    )
    new_image = jump(new_flexed, match)
    beta = new_dot / res_dot
    rhs = new_rhs + beta * rhs
    energy = new_energy + beta * (2.0 * cross + beta * energy)
    correction, coarse_energy = coarse(rhs)
    step = new_dot / (energy + coarse_energy)
    multipliers = multipliers + step * (precond + beta * direction)
    residual = residual - step * (new_image + beta * image + correction)
    return (multipliers[None, None], residual[None, None])


def solution(mesh):
    return jax.shard_map(
        shards,
        mesh=mesh,
        in_specs=(
            P("sx", "sy", None, None),
            P("sx", "sy", None, None),
            P("sx", "sy", None, None),
            P("sx", "sy", None, None),
            P("sx", "sy", None),
            P("sx", "sy", None, None),
            P(("sx", "sy"), None),
        ),
        out_specs=(P("sx", "sy", None, None), P("sx", "sy", None, None)),
        check_vma=False,
    )
```

```python
import jax
import jax.numpy as jnp
from jax import lax
from jax.experimental import pallas as pl
from jax.experimental.pallas import tpu as pltpu
from jax.sharding import PartitionSpec as P

HIGH = lax.Precision.HIGH
HIGHEST = lax.Precision.HIGHEST


def shifted(block, axis, distance):
    devices = range(lax.axis_size(axis))
    route = [(i - distance, i) for i in devices if i - distance in devices]
    return lax.ppermute(block, axis, route)


def facing(faces):
    return (
        shifted(faces[1], "sx", 1),
        shifted(faces[0], "sx", -1),
        shifted(faces[3], "sy", 1),
        shifted(faces[2], "sy", -1),
    )


def exchange_kernel(faces_ref, out_ref, held, send, recv, local):
    sx = lax.axis_index("sx")
    sy = lax.axis_index("sy")
    devices = [((sx + 7) % 8, sy), ((sx + 1) % 8, sy), (sx, (sy + 15) % 16), (sx, (sy + 1) % 16)]
    barrier = pltpu.get_barrier_semaphore()
    for device in devices:
        pl.semaphore_signal(barrier, inc=1, device_id=device, device_id_type=pl.DeviceIdType.MESH)
    pl.semaphore_wait(barrier, 4)
    copies = []
    for face in (3, 2, 1, 0):
        copy = pltpu.make_async_remote_copy(
            src_ref=faces_ref.at[face],
            dst_ref=held.at[face ^ 1],
            send_sem=send.at[face],
            recv_sem=recv.at[face],
            device_id=devices[face],
            device_id_type=pl.DeviceIdType.MESH,
        )
        copy.start()
        copies.append(copy)
    for copy in copies:
        copy.wait_recv()
    out = pltpu.make_async_copy(held, out_ref, local.at[0])
    out.start()
    out.wait()
    for copy in copies:
        copy.wait_send()


def exchanged(faces):
    return pl.pallas_call(
        exchange_kernel,
        out_shape=jax.ShapeDtypeStruct(faces.shape, faces.dtype),
        in_specs=[pl.BlockSpec(memory_space=pltpu.VMEM)],
        out_specs=pl.BlockSpec(memory_space=pl.ANY),
        scratch_shapes=[
            pltpu.VMEM(faces.shape, faces.dtype),
            pltpu.SemaphoreType.DMA((4,)),
            pltpu.SemaphoreType.DMA((4,)),
            pltpu.SemaphoreType.DMA((1,)),
        ],
        compiler_params=pltpu.CompilerParams(collective_id=1, has_side_effects=True),
        cost_estimate=pl.CostEstimate(flops=0, bytes_accessed=40_000_000, transcendentals=0),
    )(faces)


def jump(field, match, beside=False):
    size = field.shape[0] // 4
    faces = [field[f * size : (f + 1) * size] for f in range(4)]
    received = facing(faces) if beside else exchanged(field.reshape(4, size, field.shape[1]))
    return jnp.concatenate(
        [faces[f] - jnp.dot(match[f], received[f], precision=HIGHEST) for f in range(4)], axis=0
    )


def inner(first, second):
    return jnp.sum(first * second, axis=0)


def gather_kernel(block_ref, out_ref, held, send, recv, local):
    sx = lax.axis_index("sx")
    sy = lax.axis_index("sy")
    y, core = sx // 2, sx % 2
    x, z = sy // 4, sy % 4
    above, below, across = (y + 1) % 4, (y + 3) % 4, (y + 2) % 4
    sibling = (y * 2 + 1 - core, sy)
    along_x = [(sx, ((x + k) % 4) * 4 + z) for k in (1, 2, 3)]
    along_z = [(sx, x * 4 + (z + k) % 4) for k in (1, 2, 3)]
    up, down = (above * 2 + core, sy), (below * 2 + core, sy)

    partners = along_x + along_z + [up, down, sibling]
    barrier = pltpu.get_barrier_semaphore()
    for device in partners:
        pl.semaphore_signal(barrier, inc=1, device_id=device, device_id_type=pl.DeviceIdType.MESH)
    pl.semaphore_wait(barrier, len(partners))

    started = []

    def push(source, target, device):
        slot = len(started)
        copy = pltpu.make_async_remote_copy(
            src_ref=source,
            dst_ref=target,
            send_sem=send.at[slot],
            recv_sem=recv.at[slot],
            device_id=device,
            device_id_type=pl.DeviceIdType.MESH,
        )
        copy.start()
        started.append(copy)
        return copy

    keep = pltpu.make_async_copy(block_ref, held.at[core, y, z, x], local.at[0])
    keep.start()
    for copy in [push(block_ref, held.at[core, y, z, x], device) for device in along_x]:
        copy.wait_recv()
    keep.wait()
    row = held.at[core, y, z]
    for copy in [push(row, row, device) for device in along_z]:
        copy.wait_recv()
    plane = held.at[core, y]
    from_below = push(plane, plane, up)
    from_above = push(plane, plane, down)
    others = [push(plane, plane, sibling)]
    from_below.wait_recv()
    half = held.at[core, below, pl.ds(0, 2)]
    first = push(half, half, up)
    plane = held.at[core, below]
    others.append(push(plane, plane, sibling))
    from_above.wait_recv()
    half = held.at[core, above, pl.ds(2, 2)]
    second = push(half, half, down)
    plane = held.at[core, above]
    others.append(push(plane, plane, sibling))
    first.wait_recv()
    second.wait_recv()
    plane = held.at[core, across]
    others.append(push(plane, plane, sibling))
    for copy in others:
        copy.wait_recv()
    out = pltpu.make_async_copy(held, out_ref, local.at[1])
    out.start()
    out.wait()
    for copy in started:
        copy.wait_send()


def gathered(block):
    shape = (2, 4, 4, 4) + block.shape
    copies = 14
    return pl.pallas_call(
        gather_kernel,
        out_shape=jax.ShapeDtypeStruct(shape, block.dtype),
        in_specs=[pl.BlockSpec(memory_space=pltpu.VMEM)],
        out_specs=pl.BlockSpec(memory_space=pl.ANY),
        scratch_shapes=[
            pltpu.VMEM(shape, block.dtype),
            pltpu.SemaphoreType.DMA((copies,)),
            pltpu.SemaphoreType.DMA((copies,)),
            pltpu.SemaphoreType.DMA((2,)),
        ],
        compiler_params=pltpu.CompilerParams(collective_id=0, has_side_effects=True),
        cost_estimate=pl.CostEstimate(flops=0, bytes_accessed=100_000_000, transcendentals=0),
    )(block)


def shards(loads, schur_flex, dirichlet, coupling, corner_index, face_lists, coarse_inverse):
    flex_mat = schur_flex[0, 0]
    prec_mat = dirichlet[0, 0]
    coupling_mat = coupling[0, 0]
    corners = corner_index[0, 0]
    face_index = face_lists[0, 0]
    ncoarse = coarse_inverse.shape[1]
    ncl = corners.shape[0]
    size = face_index.shape[1]
    sx = lax.axis_index("sx")
    sy = lax.axis_index("sy")
    inside = jnp.stack([sx > 0, sx < lax.axis_size("sx") - 1, sy > 0, sy < lax.axis_size("sy") - 1])
    scale = jnp.repeat(1.0 + inside.astype(jnp.float32), size)[:, None]
    match = (face_index[:, :, None] == jnp.arange(size, dtype=jnp.int32)[None, None, :]).astype(jnp.float32)
    match = match * inside.astype(jnp.float32)[:, None, None]
    mine = jnp.pad(corners.astype(jnp.float32), (0, ncoarse - ncl))[None]
    everyone = lax.all_gather(jnp.concatenate([coarse_inverse, mine], axis=0), ("sx", "sy"), axis=0)
    inverse = everyone[:, :-1].reshape(ncoarse, ncoarse)

    listed = everyone[:, -1, :ncl].reshape(4, 2, 4, 4, ncl).transpose(1, 0, 3, 2, 4).reshape(-1, ncl)
    extra = jnp.array([1, 2, 3, 0, 0, 0, 0, 0], jnp.float32) + ncoarse
    slots = jnp.concatenate([listed, jnp.broadcast_to(extra, (listed.shape[0], 8))], axis=1).reshape(-1)
    place = (slots[None, :] == jnp.arange(ncoarse + 8, dtype=jnp.float32)[:, None]).astype(jnp.float32)

    coarse_ids = jnp.arange(ncoarse, dtype=jnp.float32)[None, :]
    own = corners.astype(jnp.float32)
    parts = [coupling_mat[:, f * size : (f + 1) * size].T for f in range(4)]
    tagged = [jnp.concatenate([part, jnp.broadcast_to(own, (8, ncl))], axis=0) for part in parts]
    pick = (own[:, None] == coarse_ids).astype(jnp.float32)
    columns = []
    for f, got in enumerate(facing(tagged)):
        their_pick = (got[size][:, None] == coarse_ids).astype(jnp.float32)
        theirs = jnp.dot(match[f], got[:size], precision=HIGHEST)
        columns.append(
            jnp.dot(parts[f], pick, precision=HIGHEST) - jnp.dot(theirs, their_pick, precision=HIGHEST)
        )
    coupling_jump = jnp.concatenate(columns, axis=0)

    def reduced(local_load, *rows):
        rows = list(rows) + [jnp.zeros_like(rows[0])] * (8 - len(rows))
        block = jnp.concatenate([local_load] + [row[None] for row in rows], axis=0)
        blocks = gathered(block).reshape(-1, block.shape[1])
        total = jnp.dot(place, blocks, precision=HIGHEST)
        return total[:ncoarse], total[ncoarse + 1], total[ncoarse + 2], total[ncoarse + 3]

    def coarse(rhs):
        sol = jnp.dot(inverse, rhs, precision=HIGHEST)
        return jnp.dot(coupling_jump, sol, precision=HIGHEST), inner(rhs, sol)

    def precondition(residual):
        spread = scale * residual
        applied = jnp.dot(prec_mat, spread, precision=HIGH)
        return 0.5 * jump(applied, match), 0.5 * inner(spread, applied)

    def flexible(direction):
        spread = scale * direction
        return spread, jnp.dot(flex_mat, spread, precision=HIGH), jnp.dot(coupling_mat, spread, precision=HIGH)

    residual = jump(loads[0, 0], match)
    direction, dot_part = precondition(residual)
    spread, flexed, load = flexible(direction)
    rhs, res_dot, energy, _ = reduced(load, dot_part, inner(spread, flexed))
    image = jump(flexed, match, beside=True)
    correction, coarse_energy = coarse(rhs)
    step = res_dot / (energy + coarse_energy)
    residual = residual - step * (image + correction)
    multipliers = step * direction

    precond, dot_part = precondition(residual)
    spread, new_flexed, load = flexible(precond)
    new_rhs, new_dot, new_energy, cross = reduced(
        load, dot_part, inner(spread, new_flexed), inner(spread, flexed)
    )
    new_image = jump(new_flexed, match, beside=True)
    beta = new_dot / res_dot
    rhs = new_rhs + beta * rhs
    energy = new_energy + beta * (2.0 * cross + beta * energy)
    correction, coarse_energy = coarse(rhs)
    step = new_dot / (energy + coarse_energy)
    multipliers = multipliers + step * (precond + beta * direction)
    residual = residual - step * (new_image + beta * image + correction)
    return (multipliers[None, None], residual[None, None])


def solution(mesh):
    return jax.shard_map(
        shards,
        mesh=mesh,
        in_specs=(
            P("sx", "sy", None, None),
            P("sx", "sy", None, None),
            P("sx", "sy", None, None),
            P("sx", "sy", None, None),
            P("sx", "sy", None),
            P("sx", "sy", None, None),
            P(("sx", "sy"), None),
        ),
        out_specs=(P("sx", "sy", None, None), P("sx", "sy", None, None)),
        check_vma=False,
    )
```
